32 devices in a mesh: row: 8 (over z, y), col: 4 (over x, core).
Axes of the slice: x: 2, y: 2, z: 4, core: 2. Of those that a mesh axis runs over, the one named last changes fastest.
Arguments:
- front: bfloat16 [2, 16384, 3072], P(None, 'row', 'col'), may hold values from -6 to 6
- child_tiles: bfloat16 [4096, 2, 128, 128], P(('row', 'col')), may hold values from -6 to 6
- tile_owner: int32 [4096, 1], P(('row', 'col')), may hold values from 0 to 31; in each aligned block of 128 rows (0 to 127, 128 to 255, ...) at most 8 rows name the same one
- tile_spot: int32 [4096], P(('row', 'col')), may hold values from 0 to 95
- tile_count: int32 [32], P(('row', 'col')), may hold values from 96 to 128, as said below
- panel: bfloat16 [2, 16384, 512], P(None, 'row'), may hold values from -0.03125 to 0.03125
Outputs:
- assembled: bfloat16 [2, 16384, 3072], P(None, 'row', 'col')
- sample: float32 [2, 512, 3072], P(None, 'row', 'col')
The draws below stay inside these ranges and needn't reach their ends.
Inputs may be any that keep to these rules, and one draw needn't show every extreme that they name: `tile_owner`: among the 128 tiles of one device, at most 8 name the same owner. `tile_count`: some device holds 128 live tiles.
All inputs are finite; a program needn't handle non-finite values.
Results may differ from the reference program's by a relative error of at most 0.0042.
Values may be sent and summed in bfloat16 or wider, within the bound.
A program may use at most 256 MiB of HBM per device.

```python
import math
import jax
import jax.numpy as jnp
import numpy as np
from jax import lax

TILE = 128
BR_DEV = 16
BC_DEV = 6
P_SIZE = 512
TILES_DEV = 128
NDEV = 32
CAP = 8
ROWS = 16384
COLS = 3072
N_COL = 4


def draw_tile_count(key, part):
    lowest = TILES_DEV - TILES_DEV // 4
    counts = jax.random.randint(jax.random.fold_in(key, 11), (NDEV,), lowest, TILES_DEV + 1, dtype=jnp.int32)
    fullest = jax.random.randint(jax.random.fold_in(key, 12), (), 0, NDEV, dtype=jnp.int32)
    return counts.at[fullest].set(TILES_DEV)


def set_ends(drawn, stream_key, smallest, top_value):
    longest = drawn.shape.index(max(drawn.shape))
    spots = []
    for shift in (0, 1):
        where = [jax.random.randint(jax.random.fold_in(stream_key, axis), (), 0, length) for axis, length in enumerate(drawn.shape)]
        where[longest] = (where[longest] + shift) % drawn.shape[longest]
        spots.append(tuple(where))
    return drawn.at[spots[0]].set(smallest).at[spots[1]].set(top_value)


def level_of(stream_key, shape, pieces, smallest, high):
    def one(dim, shards_of):
        draws = jax.random.uniform(jax.random.fold_in(jax.random.fold_in(stream_key, 6), dim), (shards_of,), jnp.float32, smallest / len(pieces), high / len(pieces))
        return jnp.repeat(jnp.exp(draws), shape[dim] // shards_of).reshape((-1,) + (1,) * (len(shape) - dim - 1))

    loudness = one(*pieces[0])
    for cut in pieces[1:]:
        loudness = loudness * one(*cut)
    return loudness


def routed_block(rng, own, number, rows, amount, top, reach, lean):
    order = jax.random.permutation(rng, amount)
    crowded, ordinary = load_shares(amount, rows * top, reach, lean, True), load_shares(amount, rows * top, reach, lean, False)
    places = jnp.arange(amount)

    def named(tallies, offset_by):
        used = int((tallies > 0).sum())
        fixed = max(1, used // 4)
        moved = fixed + (places - fixed + offset_by * (used - fixed)) % max(1, amount - fixed)
        return jnp.zeros((amount,), jnp.int32).at[order[jnp.where(places < fixed, places, moved)]].set(jnp.asarray(tallies, jnp.int32))

    tallies = jnp.where(number % 4 == 0, named(crowded, number // 4), named(ordinary, number - number // 4 - 1))
    mixed = jax.random.permutation(jax.random.fold_in(own, 3), amount)
    donor, sink = mixed[0:amount // 2 * 2:2], mixed[1:amount // 2 * 2:2]
    slack = jnp.minimum(tallies[donor] - 1, reach - tallies[sink]) // 2
    slack = jnp.where((donor == order[0]) | (sink == order[0]) | (tallies[sink] == 0), 0, jnp.maximum(slack, 0))
    moved = jax.random.randint(jax.random.fold_in(own, 4), (amount // 2,), 0, 1 << 20) % (slack + 1)
    tallies = tallies.at[donor].add(-moved).at[sink].add(moved)
    items = jnp.searchsorted(jnp.cumsum(tallies), jnp.arange(rows * top), side="right").astype(jnp.int32)
    grid = items.reshape(top, rows).T
    grid = grid[jax.random.permutation(jax.random.fold_in(own, 1), rows)]
    offset_by = jax.random.randint(jax.random.fold_in(own, 2), (rows, 1), 0, top)
    return jnp.take_along_axis(grid, (jnp.arange(top)[None, :] + offset_by) % top, axis=1)


def load_shares(count, total, reach, slope, full):
    weights = [(1 << 20) // math.isqrt(grade ** slope) + 1 for grade in range(1, count + 1)]
    largest = reach if full else min(reach, max(-(-total // count), total * weights[0] // sum(weights)))
    least = 1 if total - largest >= count - 1 else 0
    given, rest = [largest] + [least] * (count - 1), total - largest - least * (count - 1)
    while rest > 0:
        free = [i for i in range(1, count) if given[i] < largest] or [i for i in range(1, count) if given[i] < reach]
        whole, budget = sum([weights[i] for i in free]), rest
        for i in free:
            addition = min(reach - given[i], max(1, budget * weights[i] // whole), rest)
            given[i] = given[i] + addition
            rest = rest - addition
    return np.array(given)


def centred(key, shape, deviation, reach, cuts=(), kind=jnp.bfloat16):
    loudness = level_of(key, shape, cuts, -0.22, 0.18) if cuts else 1.0
    entries = jax.random.normal(key, shape, jnp.float32) * deviation * loudness
    return jnp.minimum(jnp.maximum(entries, -reach), reach).astype(kind)


def setup_inputs(seed: int = 0) -> dict:
    seeds = jax.random.split(jax.random.key(seed), 7)
    front = centred(seeds[0], (2, ROWS, COLS), 1.0, 6.0, ((1, 8), (2, 4)))
    child_tiles = centred(seeds[1], (NDEV * TILES_DEV, 2, TILE, TILE), 1.0, 6.0, ((0, 32),))
    tile_owner_keys = jax.random.split(jax.random.fold_in(seeds[2], 1), (NDEV * TILES_DEV) // TILES_DEV)
    tile_owner_turns = jax.random.permutation(jax.random.fold_in(seeds[2], 3), (NDEV * TILES_DEV) // TILES_DEV)
    tile_owner = jax.vmap(lambda own, number: routed_block(jax.random.fold_in(seeds[2], 2), own, number, TILES_DEV, NDEV, 1, CAP, 2))(tile_owner_keys, tile_owner_turns).reshape((NDEV * TILES_DEV, 1))
    tile_spot = set_ends(jax.random.randint(seeds[3], (NDEV * TILES_DEV,), 0, BR_DEV * BC_DEV), jax.random.fold_in(seeds[3], 1), 0, (BR_DEV * BC_DEV) - 1).astype(jnp.int32)
    tile_count = draw_tile_count(jax.random.fold_in(seeds[6], 71), 0)
    panel = centred(seeds[5], (2, ROWS, P_SIZE), (2 * ROWS) ** -0.5, 0.03125, ((1, 8),))
    return {"front": front, "child_tiles": child_tiles, "tile_owner": tile_owner, "tile_spot": tile_spot, "tile_count": tile_count, "panel": panel}


def reference(front, child_tiles, tile_owner, tile_spot, tile_count, panel):
    total = child_tiles.shape[0]
    index = jnp.arange(total, dtype=jnp.int32)
    device = index // TILES_DEV
    live = (index % TILES_DEV) < tile_count[device]
    owner = tile_owner[:, 0]
    block_rows = ROWS // TILE
    block_cols = COLS // TILE
    target_row = (owner // N_COL) * BR_DEV + tile_spot // BC_DEV
    target_col = (owner % N_COL) * BC_DEV + tile_spot % BC_DEV
    target_row = jnp.where(live, target_row, block_rows).astype(jnp.int32)
    accum = front.astype(jnp.float32).reshape(2, block_rows, TILE, block_cols, TILE)
    tiles = child_tiles.reshape(NDEV, TILES_DEV, 2, TILE, TILE)
    rows_each = target_row.reshape(NDEV, TILES_DEV)
    cols_each = target_col.reshape(NDEV, TILES_DEV).astype(jnp.int32)

    def add_device(carry, item):
        piece, rows_here, cols_here = item
        carry = carry.at[:, rows_here, :, cols_here, :].add(piece.astype(jnp.float32), mode="drop")
        return carry, None

    accum, unused = lax.scan(add_device, accum, (tiles, rows_each, cols_each))
    assembled = accum.reshape(2, ROWS, COLS).astype(jnp.bfloat16)
    panel_re, panel_im = panel[0], panel[1]
    front_re, front_im = assembled[0], assembled[1]
    real_part = jnp.dot(panel_re.T, front_re, preferred_element_type=jnp.float32) + jnp.dot(panel_im.T, front_im, preferred_element_type=jnp.float32)
    imag_part = jnp.dot(panel_re.T, front_im, preferred_element_type=jnp.float32) - jnp.dot(panel_im.T, front_re, preferred_element_type=jnp.float32)
    return assembled, jnp.stack([real_part, imag_part])
```

```python
import functools

import jax
import jax.numpy as jnp
from jax import lax
from jax.experimental import pallas as pl
from jax.experimental.pallas import tpu as pltpu
from jax.sharding import PartitionSpec as P

DEPTH = 16


def combine_kernel(
    order, spots, bounds, front, panel, tiles, assembled, partial, acc, held, total, sems
):
    step = pl.program_id(0)
    steps = pl.num_programs(0)
    tile = held.shape[2]
    n_here = acc.shape[0]
    cols_blocks = front.shape[2] // tile
    n_filled = bounds[steps]

    def fetch(e):
        slot = lax.rem(e, DEPTH)
        return pltpu.make_async_copy(tiles.at[order[e]], held.at[slot], sems.at[slot])

    @pl.when(step == 0)
    def _():
        for e in range(DEPTH):
            @pl.when(e < n_filled)
            def _():
                fetch(e).start()

    for b in range(n_here):
        r, c = b // cols_blocks, b % cols_blocks
        acc[b] = front[:, r * tile:(r + 1) * tile, c * tile:(c + 1) * tile].astype(jnp.float32)

    def add(e, carry):
        fetch(e).wait()
        slot = lax.rem(e, DEPTH)
        b = spots[e] - step * n_here
        acc[b] = acc[b] + held[slot].astype(jnp.float32)

        @pl.when(e + DEPTH < n_filled)
        def _():
            fetch(e + DEPTH).start()

        return carry

    lax.fori_loop(bounds[step], bounds[step + 1], add, 0)

    for b in range(n_here):
        r, c = b // cols_blocks, b % cols_blocks
        assembled[:, r * tile:(r + 1) * tile, c * tile:(c + 1) * tile] = acc[b].astype(
            jnp.bfloat16
        )

    @pl.when(step == 0)
    def _():
        total[...] = jnp.zeros_like(total)

    def times(a, b):
        return lax.dot_general(
            a, b, (((0,), (0,)), ((), ())), preferred_element_type=jnp.float32
        )

    total[0] += times(panel[0], assembled[0]) + times(panel[1], assembled[1])
    total[1] += times(panel[0], assembled[1]) - times(panel[1], assembled[0])

    @pl.when(step == steps - 1)
    def _():
        rows_out = partial.shape[2]
        for d in range(partial.shape[0]):
            partial[d] = total[:, d * rows_out:(d + 1) * rows_out, :].astype(jnp.bfloat16)


def combine(front, panel, tiles, order, spots, bounds, n_row, group):
    _, rows, width = front.shape
    p_size = panel.shape[2]
    tile = tiles.shape[2]
    high = group * tile
    steps = rows // high
    return pl.pallas_call(
        combine_kernel,
        grid_spec=pltpu.PrefetchScalarGridSpec(
            num_scalar_prefetch=3,
            grid=(steps,),
            in_specs=[
                pl.BlockSpec((2, high, width), lambda i, *_: (0, i, 0)),
                pl.BlockSpec((2, high, p_size), lambda i, *_: (0, i, 0)),
                pl.BlockSpec(memory_space=pl.ANY),
            ],
            out_specs=[
                pl.BlockSpec((2, high, width), lambda i, *_: (0, i, 0)),
                pl.BlockSpec((n_row, 2, p_size // n_row, width), lambda i, *_: (0, 0, 0, 0)),
            ],
            scratch_shapes=[
                pltpu.VMEM((group * (width // tile), 2, tile, tile), jnp.float32),
                pltpu.VMEM((DEPTH, 2, tile, tile), jnp.bfloat16),
                pltpu.VMEM((2, p_size, width), jnp.float32),
                pltpu.SemaphoreType.DMA((DEPTH,)),
            ],
        ),
        out_shape=[
            jax.ShapeDtypeStruct(front.shape, jnp.bfloat16),
            jax.ShapeDtypeStruct((n_row, 2, p_size // n_row, width), jnp.bfloat16),
        ],
        compiler_params=pltpu.CompilerParams(dimension_semantics=("arbitrary",)),
    )(order, spots, bounds, front, panel, tiles)


def by_spot(got_spots, n_local, per_step):
    n = got_spots.shape[0]
    index = jnp.arange(n, dtype=jnp.int32)
    ahead = (got_spots[None, :] < got_spots[:, None]) | (
        (got_spots[None, :] == got_spots[:, None]) & (index[None, :] < index[:, None])
    )
    place = jnp.sum(ahead.astype(jnp.int32), axis=1)
    at = place[None, :] == index[:, None]
    order = jnp.sum(jnp.where(at, index[None, :], 0), axis=1)
    spots = jnp.sum(jnp.where(at, got_spots[None, :], 0), axis=1)
    edges = jnp.arange(n_local // per_step + 1, dtype=jnp.int32) * per_step
    bounds = jnp.sum((got_spots[None, :] < edges[:, None]).astype(jnp.int32), axis=1)
    return order, spots, bounds


def body(front, child_tiles, tile_owner, tile_spot, tile_count, panel):
    n_row = lax.axis_size("row")
    n_col = lax.axis_size("col")
    n_dev = n_row * n_col
    n_tiles = child_tiles.shape[0]
    tile = child_tiles.shape[2]
    slots = max(2, 2 * n_tiles // n_dev)
    rows_blocks = front.shape[1] // tile
    cols_blocks = front.shape[2] // tile
    n_local = rows_blocks * cols_blocks
    group = 2 if rows_blocks % 2 == 0 else 1
    order = jnp.arange(n_tiles, dtype=jnp.int32)
    owner = tile_owner[:, 0]
    live = order < tile_count[0]
    earlier = (owner[:, None] == owner[None, :]) & live[None, :] & (order[None, :] < order[:, None])
    rank = jnp.sum(earlier.astype(jnp.int32), axis=1)
    slot = jnp.where(live, owner * slots + rank, n_dev * slots)
    here = slot[None, :] == jnp.arange(n_dev * slots, dtype=jnp.int32)[:, None]
    picked = jnp.sum(jnp.where(here, order[None, :], 0), axis=1)
    send_spots = n_local + jnp.sum(jnp.where(here, tile_spot[None, :] - n_local, 0), axis=1)
    send_tiles = child_tiles[picked]
    got_spots = lax.all_to_all(
        send_spots.reshape(n_dev, slots), ("row", "col"), split_axis=0, concat_axis=0, tiled=True
    ).reshape(n_dev * slots)
    got_tiles = lax.all_to_all(
        send_tiles.reshape(n_dev, slots, 2, tile, tile),
        ("row", "col"),
        split_axis=0,
        concat_axis=0,
        tiled=True,
    ).reshape(n_dev * slots, 2, tile, tile)
    listed, spots, bounds = by_spot(got_spots, n_local, group * cols_blocks)
    assembled, partial = combine(
        front, panel, got_tiles, listed, spots, bounds, n_row, group
    )
    parts = lax.all_to_all(partial, "row", split_axis=0, concat_axis=0, tiled=True)
    sample = jnp.sum(parts.astype(jnp.float32), axis=0)
    return (assembled, sample)


def solution(mesh):
    placed = (
        P(None, "row", "col"),
        P(("row", "col"), None, None, None),
        P(("row", "col"), None),
        P(("row", "col")),
        P(("row", "col")),
        P(None, "row", None),
    )
    return jax.shard_map(
        body,
        mesh=mesh,
        in_specs=placed,
        out_specs=(P(None, "row", "col"), P(None, "row", "col")),
        check_vma=False,
    )
```

```python
import functools

import jax
import jax.numpy as jnp
from jax import lax
from jax.experimental import pallas as pl
from jax.experimental.pallas import tpu as pltpu
from jax.sharding import PartitionSpec as P

DEPTH = 16


def combine_kernel(
    order, spots, bounds, front, panel, near, far, assembled, partial, acc, held, total, sems
):
    step = pl.program_id(0)
    steps = pl.num_programs(0)
    tile = held.shape[2]
    n_here = acc.shape[0]
    cols_blocks = front.shape[2] // tile
    n_filled = bounds[steps]

    n_near = near.shape[0]

    def fetch(e):
        slot = lax.rem(e, DEPTH)
        place = order[e]

        @pl.when(place < n_near)
        def _():
            pltpu.make_async_copy(near.at[place], held.at[slot], sems.at[slot]).start()

        @pl.when(place >= n_near)
        def _():
            pltpu.make_async_copy(far.at[place - n_near], held.at[slot], sems.at[slot]).start()

    @pl.when(step == 0)
    def _():
        for e in range(DEPTH):
            @pl.when(e < n_filled)
            def _():
                fetch(e)

    for b in range(n_here):
        r, c = b // cols_blocks, b % cols_blocks
        acc[b] = front[:, r * tile:(r + 1) * tile, c * tile:(c + 1) * tile].astype(jnp.float32)

    def add(e, carry):
        slot = lax.rem(e, DEPTH)
        pltpu.make_async_copy(near.at[0], held.at[slot], sems.at[slot]).wait()
        b = spots[e] - step * n_here
        acc[b] = acc[b] + held[slot].astype(jnp.float32)

        @pl.when(e + DEPTH < n_filled)
        def _():
            fetch(e + DEPTH)

        return carry

    lax.fori_loop(bounds[step], bounds[step + 1], add, 0)

    for b in range(n_here):
        r, c = b // cols_blocks, b % cols_blocks
        assembled[:, r * tile:(r + 1) * tile, c * tile:(c + 1) * tile] = acc[b].astype(
            jnp.bfloat16
        )

    @pl.when(step == 0)
    def _():
        total[...] = jnp.zeros_like(total)

    def times(a, b):
        return lax.dot_general(
            a, b, (((0,), (0,)), ((), ())), preferred_element_type=jnp.float32
        )

    total[0] += times(panel[0], assembled[0]) + times(panel[1], assembled[1])
    total[1] += times(panel[0], assembled[1]) - times(panel[1], assembled[0])

    @pl.when(step == steps - 1)
    def _():
        rows_out = partial.shape[2]
        for d in range(partial.shape[0]):
            partial[d] = total[:, d * rows_out:(d + 1) * rows_out, :].astype(jnp.bfloat16)


def combine(front, panel, near, far, order, spots, bounds, n_row, group):
    _, rows, width = front.shape
    p_size = panel.shape[2]
    tile = near.shape[2]
    high = group * tile
    steps = rows // high
    return pl.pallas_call(
        combine_kernel,
        grid_spec=pltpu.PrefetchScalarGridSpec(
            num_scalar_prefetch=3,
            grid=(steps,),
            in_specs=[
                pl.BlockSpec((2, high, width), lambda i, *_: (0, i, 0)),
                pl.BlockSpec((2, high, p_size), lambda i, *_: (0, i, 0)),
                pl.BlockSpec(memory_space=pl.ANY),
                pl.BlockSpec(memory_space=pl.ANY),
            ],
            out_specs=[
                pl.BlockSpec((2, high, width), lambda i, *_: (0, i, 0)),
                pl.BlockSpec((n_row, 2, p_size // n_row, width), lambda i, *_: (0, 0, 0, 0)),
            ],
            scratch_shapes=[
                pltpu.VMEM((group * (width // tile), 2, tile, tile), jnp.float32),
                pltpu.VMEM((DEPTH, 2, tile, tile), jnp.bfloat16),
                pltpu.VMEM((2, p_size, width), jnp.float32),
                pltpu.SemaphoreType.DMA((DEPTH,)),
            ],
        ),
        out_shape=[
            jax.ShapeDtypeStruct(front.shape, jnp.bfloat16),
            jax.ShapeDtypeStruct((n_row, 2, p_size // n_row, width), jnp.bfloat16),
        ],
        compiler_params=pltpu.CompilerParams(dimension_semantics=("arbitrary",)),
    )(order, spots, bounds, front, panel, near, far)


def by_spot(got_spots, n_local, per_step):
    n = got_spots.shape[0]
    index = jnp.arange(n, dtype=jnp.int32)
    ahead = (got_spots[None, :] < got_spots[:, None]) | (
        (got_spots[None, :] == got_spots[:, None]) & (index[None, :] < index[:, None])
    )
    place = jnp.sum(ahead.astype(jnp.int32), axis=1)
    at = place[None, :] == index[:, None]
    order = jnp.sum(jnp.where(at, index[None, :], 0), axis=1)
    spots = jnp.sum(jnp.where(at, got_spots[None, :], 0), axis=1)
    edges = jnp.arange(n_local // per_step + 1, dtype=jnp.int32) * per_step
    bounds = jnp.sum((got_spots[None, :] < edges[:, None]).astype(jnp.int32), axis=1)
    return order, spots, bounds


def swap_kernel(n_half, n_col, slots, length, *refs):
    if length:
        send, got, mirrored, send_sems, recv_sems = refs
    else:
        send, got, send_sems, recv_sems = refs
    row, col = lax.axis_index("row"), lax.axis_index("col")
    half_rows = n_half // n_col
    half = row // half_rows
    k = lax.rem(row, half_rows) * n_col + col

    def peer(j):
        return lax.rem(k + j, n_half)

    def device(p):
        return (half * half_rows + p // n_col, lax.rem(p, n_col))

    across = (lax.rem(row + half_rows, 2 * half_rows), col)
    mesh_id = pl.DeviceIdType.MESH
    barrier = pltpu.get_barrier_semaphore()
    for j in range(1, n_half):
        pl.semaphore_signal(barrier, inc=1, device_id=device(peer(j)), device_id_type=mesh_id)
    if length:
        pl.semaphore_signal(barrier, inc=1, device_id=across, device_id_type=mesh_id)
    pl.semaphore_wait(barrier, n_half if length else n_half - 1)

    copies = []
    if length:
        copies.append(
            pltpu.make_async_remote_copy(
                src_ref=send.at[pl.ds(n_half * slots, length)],
                dst_ref=mirrored.at[pl.ds(0, length)],
                send_sem=send_sems.at[0],
                recv_sem=recv_sems.at[0],
                device_id=across,
                device_id_type=mesh_id,
            )
        )
    for j in range(1, n_half):
        copies.append(
            pltpu.make_async_remote_copy(
                src_ref=send.at[pl.ds(peer(j) * slots, slots)],
                dst_ref=got.at[pl.ds(k * slots, slots)],
                send_sem=send_sems.at[j],
                recv_sem=recv_sems.at[j],
                device_id=device(peer(j)),
                device_id_type=mesh_id,
            )
        )
    for copy in copies:
        copy.start()
    own = pltpu.make_async_copy(
        send.at[pl.ds(k * slots, slots)], got.at[pl.ds(k * slots, slots)], send_sems.at[n_half]
    )
    own.start()
    own.wait()
    for copy in copies:
        copy.wait()


def swap(send, n_half, n_col, slots, length, number):
    shape = jax.ShapeDtypeStruct((n_half * slots,) + send.shape[1:], send.dtype)
    count = 2 if length else 1
    return pl.pallas_call(
        functools.partial(swap_kernel, n_half, n_col, slots, length),
        in_specs=[pl.BlockSpec(memory_space=pl.ANY)],
        out_specs=[pl.BlockSpec(memory_space=pl.ANY)] * count,
        out_shape=[shape] * count,
        scratch_shapes=[
            pltpu.SemaphoreType.DMA((n_half + 1,)),
            pltpu.SemaphoreType.DMA((n_half,)),
        ],
        compiler_params=pltpu.CompilerParams(collective_id=number, has_side_effects=True),
    )(send)


def body(front, child_tiles, tile_owner, tile_spot, tile_count, panel):
    n_row = lax.axis_size("row")
    n_col = lax.axis_size("col")
    n_dev = n_row * n_col
    n_half = n_dev // 2
    n_tiles = child_tiles.shape[0]
    tile = child_tiles.shape[2]
    slots = max(2, 2 * n_tiles // n_dev)
    room = n_half * slots
    rows_blocks = front.shape[1] // tile
    cols_blocks = front.shape[2] // tile
    n_local = rows_blocks * cols_blocks
    group = 2 if rows_blocks % 2 == 0 else 1
    half = lax.axis_index("row") // (n_row // 2)
    mine = lax.rem(lax.axis_index("row"), n_row // 2) * n_col + lax.axis_index("col")
    order = jnp.arange(n_tiles, dtype=jnp.int32)
    devices = jnp.arange(n_dev, dtype=jnp.int32)
    places = jnp.arange(n_half, dtype=jnp.int32)
    rows = jnp.arange(2 * room, dtype=jnp.int32)
    owner = tile_owner[:, 0]
    live = order < tile_count[0]
    is_far = live & (owner // n_half != half)
    earlier = (owner[:, None] == owner[None, :]) & live[None, :] & (order[None, :] < order[:, None])
    rank = jnp.sum(earlier.astype(jnp.int32), axis=1)
    below = jnp.sum(
        (is_far[None, :] & (owner[None, :] < owner[:, None])).astype(jnp.int32), axis=1
    )
    spread = jnp.where(live, owner * slots + rank, 2 * room)
    packed = jnp.where(
        is_far, room + below + rank, lax.rem(owner, n_half) * slots + rank
    )
    packed = jnp.where(live, packed, 2 * room)
    picked = jnp.sum(jnp.where(packed[None, :] == rows[:, None], order[None, :], 0), axis=1)
    send_spots = n_local + jnp.sum(
        jnp.where(spread[None, :] == rows[:, None], tile_spot[None, :] - n_local, 0), axis=1
    )
    far_owner = jnp.where(is_far, lax.rem(owner, n_half), n_half)
    far_counts = jnp.sum((far_owner[None, :] == places[:, None]).astype(jnp.int32), axis=1)
    news = jnp.concatenate(
        [
            send_spots.reshape(n_dev, slots),
            jnp.broadcast_to(far_counts[None, :], (n_dev, n_half)),
        ],
        axis=1,
    )
    heard = lax.all_to_all(news, ("row", "col"), split_axis=0, concat_axis=0, tiled=True)
    send = child_tiles[picked]
    fullest = jnp.max(jnp.sum(heard[:, slots:], axis=1))
    levels = sorted({-(-room * part // 16) for part in (9, 10, 16)})
    level = sum((fullest > size).astype(jnp.int32) for size in levels[:-1])
    near, mirrored = lax.switch(
        level,
        [
            functools.partial(
                lambda size, number, s: tuple(swap(s, n_half, n_col, slots, size, number)),
                size,
                number,
            )
            for number, size in enumerate(levels)
        ],
        send,
    )
    across = (1 - half) * n_half + mine
    theirs = jnp.sum(
        jnp.where(devices[:, None] == across, heard[:, slots:], 0), axis=0
    )
    start = jnp.sum(jnp.where(places[None, :] < places[:, None], theirs[None, :], 0), axis=1)
    ranks = jnp.arange(slots, dtype=jnp.int32)
    taken = jnp.where(ranks[None, :] < theirs[:, None], start[:, None] + ranks[None, :], 0)
    (far,) = swap(mirrored[taken.reshape(room)], n_half, n_col, slots, 0, len(levels))
    spots_in = heard[:, :slots].reshape(2, room)
    got_spots = jnp.where(half == 0, spots_in, spots_in[::-1]).reshape(2 * room)
    listed, spots, bounds = by_spot(got_spots, n_local, group * cols_blocks)
    assembled, partial = combine(
        front, panel, near, far, listed, spots, bounds, n_row, group
    )
    parts = lax.all_to_all(partial, "row", split_axis=0, concat_axis=0, tiled=True)
    sample = jnp.sum(parts.astype(jnp.float32), axis=0)
    return (assembled, sample)


def solution(mesh):
    placed = (
        P(None, "row", "col"),
        P(("row", "col"), None, None, None),
        P(("row", "col"), None),
        P(("row", "col")),
        P(("row", "col")),
        P(None, "row", None),
    )
    return jax.shard_map(
        body,
        mesh=mesh,
        in_specs=placed,
        out_specs=(P(None, "row", "col"), P(None, "row", "col")),
        check_vma=False,
    )
```

```python
import functools

import jax
import jax.numpy as jnp
from jax import lax
from jax.experimental import pallas as pl
from jax.experimental.pallas import tpu as pltpu
from jax.sharding import PartitionSpec as P

DEPTH = 16


def combine_kernel(
    order, spots, bounds, front, panel, near, crossed, passed, assembled, partial, acc, held, total, sems
):
    step = pl.program_id(0)
    steps = pl.num_programs(0)
    tile = held.shape[2]
    n_here = acc.shape[0]
    cols_blocks = front.shape[2] // tile
    n_filled = bounds[steps]

    sources, first = [], 0
    for source in (near, crossed, passed):
        sources.append((source, first))
        first += source.shape[0]

    def fetch(e):
        slot = lax.rem(e, DEPTH)
        place = order[e]
        for source, first in sources:
            @pl.when((place >= first) & (place < first + source.shape[0]))
            def _():
                pltpu.make_async_copy(
                    source.at[place - first], held.at[slot], sems.at[slot]
                ).start()

    @pl.when(step == 0)
    def _():
        for e in range(DEPTH):
            @pl.when(e < n_filled)
            def _():
                fetch(e)

    for b in range(n_here):
        r, c = b // cols_blocks, b % cols_blocks
        acc[b] = front[:, r * tile:(r + 1) * tile, c * tile:(c + 1) * tile].astype(jnp.float32)

    def add(e, carry):
        slot = lax.rem(e, DEPTH)
        pltpu.make_async_copy(near.at[0], held.at[slot], sems.at[slot]).wait()
        b = spots[e] - step * n_here
        acc[b] = acc[b] + held[slot].astype(jnp.float32)

        @pl.when(e + DEPTH < n_filled)
        def _():
            fetch(e + DEPTH)

        return carry

    lax.fori_loop(bounds[step], bounds[step + 1], add, 0)

    for b in range(n_here):
        r, c = b // cols_blocks, b % cols_blocks
        assembled[:, r * tile:(r + 1) * tile, c * tile:(c + 1) * tile] = acc[b].astype(
            jnp.bfloat16
        )

    @pl.when(step == 0)
    def _():
        total[...] = jnp.zeros_like(total)

    def times(a, b):
        return lax.dot_general(
            a, b, (((0,), (0,)), ((), ())), preferred_element_type=jnp.float32
        )

    total[0] += times(panel[0], assembled[0]) + times(panel[1], assembled[1])
    total[1] += times(panel[0], assembled[1]) - times(panel[1], assembled[0])

    @pl.when(step == steps - 1)
    def _():
        rows_out = partial.shape[2]
        for d in range(partial.shape[0]):
            partial[d] = total[:, d * rows_out:(d + 1) * rows_out, :].astype(jnp.bfloat16)


def combine(front, panel, near, crossed, passed, order, spots, bounds, n_row, group):
    _, rows, width = front.shape
    p_size = panel.shape[2]
    tile = near.shape[2]
    high = group * tile
    steps = rows // high
    return pl.pallas_call(
        combine_kernel,
        grid_spec=pltpu.PrefetchScalarGridSpec(
            num_scalar_prefetch=3,
            grid=(steps,),
            in_specs=[
                pl.BlockSpec((2, high, width), lambda i, *_: (0, i, 0)),
                pl.BlockSpec((2, high, p_size), lambda i, *_: (0, i, 0)),
                pl.BlockSpec(memory_space=pl.ANY),
                pl.BlockSpec(memory_space=pl.ANY),
                pl.BlockSpec(memory_space=pl.ANY),
            ],
            out_specs=[
                pl.BlockSpec((2, high, width), lambda i, *_: (0, i, 0)),
                pl.BlockSpec((n_row, 2, p_size // n_row, width), lambda i, *_: (0, 0, 0, 0)),
            ],
            scratch_shapes=[
                pltpu.VMEM((group * (width // tile), 2, tile, tile), jnp.float32),
                pltpu.VMEM((DEPTH, 2, tile, tile), jnp.bfloat16),
                pltpu.VMEM((2, p_size, width), jnp.float32),
                pltpu.SemaphoreType.DMA((DEPTH,)),
            ],
        ),
        out_shape=[
            jax.ShapeDtypeStruct(front.shape, jnp.bfloat16),
            jax.ShapeDtypeStruct((n_row, 2, p_size // n_row, width), jnp.bfloat16),
        ],
        compiler_params=pltpu.CompilerParams(dimension_semantics=("arbitrary",)),
    )(order, spots, bounds, front, panel, near, crossed, passed)


def by_spot(got_spots, n_local, per_step):
    n = got_spots.shape[0]
    index = jnp.arange(n, dtype=jnp.int32)
    ahead = (got_spots[None, :] < got_spots[:, None]) | (
        (got_spots[None, :] == got_spots[:, None]) & (index[None, :] < index[:, None])
    )
    place = jnp.sum(ahead.astype(jnp.int32), axis=1)
    at = place[None, :] == index[:, None]
    order = jnp.sum(jnp.where(at, index[None, :], 0), axis=1)
    spots = jnp.sum(jnp.where(at, got_spots[None, :], 0), axis=1)
    edges = jnp.arange(n_local // per_step + 1, dtype=jnp.int32) * per_step
    bounds = jnp.sum((got_spots[None, :] < edges[:, None]).astype(jnp.int32), axis=1)
    return order, spots, bounds


def peers_in_turn(n):
    return sorted(range(1, n), key=lambda j: (bin(j).count("1"), -j))


def swap_kernel(n_half, n_col, slots, direct, length, *refs):
    if length:
        send, got, crossed, mirrored, send_sems, recv_sems = refs
    else:
        send, got, send_sems, recv_sems = refs
    row, col = lax.axis_index("row"), lax.axis_index("col")
    half_rows = n_half // n_col
    half = row // half_rows
    k = lax.rem(row, half_rows) * n_col + col
    even = n_half & (n_half - 1) == 0

    def peer(j):
        if not even:
            return lax.rem(k + j, n_half)
        place = k
        for b in range(n_half.bit_length() - 1):
            if j >> b & 1:
                place = place + (1 << b) * (1 - 2 * ((k // (1 << b)) % 2))
        return place

    def device(side, p):
        return (side * half_rows + p // n_col, lax.rem(p, n_col))

    mesh_id = pl.DeviceIdType.MESH
    barrier = pltpu.get_barrier_semaphore()
    for j in range(1, n_half):
        pl.semaphore_signal(
            barrier, inc=1, device_id=device(half, peer(j)), device_id_type=mesh_id
        )
    if length:
        for j in range(n_half):
            pl.semaphore_signal(
                barrier, inc=1, device_id=device(1 - half, peer(j)), device_id_type=mesh_id
            )
    pl.semaphore_wait(barrier, 2 * n_half - 1 if length else n_half - 1)

    copies = []

    def post(source, target, number, to):
        copies.append(
            pltpu.make_async_remote_copy(
                src_ref=source,
                dst_ref=target,
                send_sem=send_sems.at[number],
                recv_sem=recv_sems.at[number],
                device_id=to,
                device_id_type=mesh_id,
            )
        )

    turn = peers_in_turn(n_half)
    if length:
        base = n_half * slots
        post(
            send.at[pl.ds(base + n_half * direct, length)],
            mirrored.at[pl.ds(0, length)],
            0,
            device(1 - half, k),
        )
        for j in [0] + turn:
            post(
                send.at[pl.ds(base + peer(j) * direct, direct)],
                crossed.at[pl.ds(k * direct, direct)],
                n_half + j,
                device(1 - half, peer(j)),
            )
    for j in turn:
        post(
            send.at[pl.ds(peer(j) * slots, slots)],
            got.at[pl.ds(k * slots, slots)],
            j,
            device(half, peer(j)),
        )
    for copy in copies:
        copy.start()
    own = pltpu.make_async_copy(
        send.at[pl.ds(k * slots, slots)],
        got.at[pl.ds(k * slots, slots)],
        send_sems.at[2 * n_half],
    )
    own.start()
    own.wait()
    for copy in copies:
        copy.wait()


def swap(send, n_half, n_col, slots, direct, room, length, number):
    def shape(rows):
        return jax.ShapeDtypeStruct((rows,) + send.shape[1:], send.dtype)

    shapes = [shape(n_half * slots)]
    if length:
        shapes += [shape(n_half * direct), shape(room)]
    return pl.pallas_call(
        functools.partial(swap_kernel, n_half, n_col, slots, direct, length),
        in_specs=[pl.BlockSpec(memory_space=pl.ANY)],
        out_specs=[pl.BlockSpec(memory_space=pl.ANY)] * len(shapes),
        out_shape=shapes,
        scratch_shapes=[
            pltpu.SemaphoreType.DMA((2 * n_half + 1,)),
            pltpu.SemaphoreType.DMA((2 * n_half,)),
        ],
        compiler_params=pltpu.CompilerParams(collective_id=number, has_side_effects=True),
    )(send)


def fold_kernel(n_row, part, out, sums, landed, send_sems, recv_sems):
    row, col = lax.axis_index("row"), lax.axis_index("col")
    bits = n_row.bit_length() - 1
    width = part.shape[3]

    def flip(t):
        place = row
        for b in range(bits):
            if t >> b & 1:
                place = place + (1 << b) * (1 - 2 * ((row // (1 << b)) % 2))
        return place

    mesh_id = pl.DeviceIdType.MESH
    barrier = pltpu.get_barrier_semaphore()
    for b in range(bits):
        pl.semaphore_signal(
            barrier, inc=1, device_id=(flip(1 << b), col), device_id_type=mesh_id
        )
    pl.semaphore_wait(barrier, bits)

    orders = [list(range(bits))]
    if width % 256 == 0 and bits > 1:
        orders.append([1, 0] + list(range(2, bits)))
    span = width // len(orders)
    left = [list(range(n_row)) for _ in orders]
    parts_of = [{t: [] for t in range(n_row)} for _ in orders]
    used = 0

    def value(h, t):
        total = part[flip(t), :, :, h * span:(h + 1) * span].astype(jnp.float32)
        for slot in parts_of[h][t]:
            total = total + landed[slot].astype(jnp.float32)
        return total

    for step in range(bits):
        copies = []
        for h, order in enumerate(orders):
            bit = 1 << order[step]
            for t in [t for t in left[h] if t & bit]:
                if step == 0:
                    source = part.at[flip(t), :, :, pl.ds(h * span, span)]
                else:
                    sums[used] = value(h, t).astype(jnp.bfloat16)
                    source = sums.at[used]
                copy = pltpu.make_async_remote_copy(
                    src_ref=source,
                    dst_ref=landed.at[used],
                    send_sem=send_sems.at[used],
                    recv_sem=recv_sems.at[used],
                    device_id=(flip(bit), col),
                    device_id_type=mesh_id,
                )
                copy.start()
                copies.append((copy, h, t ^ bit, used))
                used += 1
            left[h] = [t for t in left[h] if not t & bit]
        for copy, h, t, slot in copies:
            copy.wait()
            parts_of[h][t].append(slot)
    for h in range(len(orders)):
        out[:, :, h * span:(h + 1) * span] = value(h, 0)


def fold(partial, n_row, number):
    _, _, rows_out, width = partial.shape
    halves = 2 if width % 256 == 0 and n_row > 2 else 1
    count = halves * (n_row - 1)
    block = (count, 2, rows_out, width // halves)
    return pl.pallas_call(
        functools.partial(fold_kernel, n_row),
        in_specs=[pl.BlockSpec(memory_space=pltpu.VMEM)],
        out_specs=pl.BlockSpec(memory_space=pltpu.VMEM),
        out_shape=jax.ShapeDtypeStruct((2, rows_out, width), jnp.float32),
        scratch_shapes=[
            pltpu.VMEM(block, jnp.bfloat16),
            pltpu.VMEM(block, jnp.bfloat16),
            pltpu.SemaphoreType.DMA((count,)),
            pltpu.SemaphoreType.DMA((count,)),
        ],
        compiler_params=pltpu.CompilerParams(collective_id=number, has_side_effects=True),
    )(partial)


def body(front, child_tiles, tile_owner, tile_spot, tile_count, panel):
    n_row = lax.axis_size("row")
    n_col = lax.axis_size("col")
    n_dev = n_row * n_col
    n_half = n_dev // 2
    n_tiles = child_tiles.shape[0]
    tile = child_tiles.shape[2]
    slots = max(2, 2 * n_tiles // n_dev)
    direct = slots // 2
    beyond = slots - direct
    room = n_half * beyond
    near_rows = n_half * slots
    far_rows = n_half * direct
    rows_blocks = front.shape[1] // tile
    cols_blocks = front.shape[2] // tile
    n_local = rows_blocks * cols_blocks
    group = 2 if rows_blocks % 2 == 0 else 1
    half = lax.axis_index("row") // (n_row // 2)
    mine = lax.rem(lax.axis_index("row"), n_row // 2) * n_col + lax.axis_index("col")
    order = jnp.arange(n_tiles, dtype=jnp.int32)
    devices = jnp.arange(n_dev, dtype=jnp.int32)
    places = jnp.arange(n_half, dtype=jnp.int32)
    rows = jnp.arange(2 * near_rows, dtype=jnp.int32)
    owner = tile_owner[:, 0]
    live = order < tile_count[0]
    is_far = live & (owner // n_half != half)
    earlier = (owner[:, None] == owner[None, :]) & live[None, :] & (order[None, :] < order[:, None])
    rank = jnp.sum(earlier.astype(jnp.int32), axis=1)
    is_over = is_far & (rank >= direct)
    below = jnp.sum(
        (is_over[None, :] & (owner[None, :] < owner[:, None])).astype(jnp.int32), axis=1
    )
    spread = jnp.where(live, owner * slots + rank, 2 * near_rows)
    place = lax.rem(owner, n_half)
    packed = jnp.where(
        is_over,
        near_rows + far_rows + below + rank - direct,
        jnp.where(is_far, near_rows + place * direct + rank, place * slots + rank),
    )
    packed = jnp.where(live, packed, 2 * near_rows)
    picked = jnp.sum(jnp.where(packed[None, :] == rows[:, None], order[None, :], 0), axis=1)
    send_spots = n_local + jnp.sum(
        jnp.where(spread[None, :] == rows[:, None], tile_spot[None, :] - n_local, 0), axis=1
    )
    far_owner = jnp.where(is_over, place, n_half)
    far_counts = jnp.sum((far_owner[None, :] == places[:, None]).astype(jnp.int32), axis=1)
    news = jnp.concatenate(
        [
            send_spots.reshape(n_dev, slots),
            jnp.broadcast_to(far_counts[None, :], (n_dev, n_half)),
        ],
        axis=1,
    )
    heard = lax.all_to_all(news, ("row", "col"), split_axis=0, concat_axis=0, tiled=True)
    send = child_tiles[picked]
    fullest = jnp.max(jnp.sum(heard[:, slots:], axis=1))
    levels = sorted({-(-room * part // 16) for part in (4, 5, 6, 8, 16)})
    level = sum((fullest > size).astype(jnp.int32) for size in levels[:-1])
    near, crossed, mirrored = lax.switch(
        level,
        [
            functools.partial(
                lambda size, number, s: tuple(
                    swap(s, n_half, n_col, slots, direct, room, size, number)
                ),
                size,
                number,
            )
            for number, size in enumerate(levels)
        ],
        send,
    )
    across = (1 - half) * n_half + mine
    theirs = jnp.sum(
        jnp.where(devices[:, None] == across, heard[:, slots:], 0), axis=0
    )
    start = jnp.sum(jnp.where(places[None, :] < places[:, None], theirs[None, :], 0), axis=1)
    ranks = jnp.arange(beyond, dtype=jnp.int32)
    taken = jnp.where(ranks[None, :] < theirs[:, None], start[:, None] + ranks[None, :], 0)
    (passed,) = swap(
        mirrored[taken.reshape(room)], n_half, n_col, beyond, direct, room, 0, len(levels)
    )
    spots_in = heard[:, :slots].reshape(2, n_half, slots)
    spots_near = jnp.where(half == 0, spots_in[0], spots_in[1])
    spots_far = jnp.where(half == 0, spots_in[1], spots_in[0])
    got_spots = jnp.concatenate(
        [
            spots_near.reshape(near_rows),
            spots_far[:, :direct].reshape(far_rows),
            spots_far[:, direct:].reshape(room),
        ]
    )
    listed, spots, bounds = by_spot(got_spots, n_local, group * cols_blocks)
    assembled, partial = combine(
        front, panel, near, crossed, passed, listed, spots, bounds, n_row, group
    )
    sample = fold(partial, n_row, len(levels) + 1)
    return (assembled, sample)


def solution(mesh):
    placed = (
        P(None, "row", "col"),
        P(("row", "col"), None, None, None),
        P(("row", "col"), None),
        P(("row", "col")),
        P(("row", "col")),
        P(None, "row", None),
    )
    return jax.shard_map(
        body,
        mesh=mesh,
        in_specs=placed,
        out_specs=(P(None, "row", "col"), P(None, "row", "col")),
        check_vma=False,
    )
```

```python
import functools

import jax
import jax.numpy as jnp
from jax import lax
from jax.experimental import pallas as pl
from jax.experimental.pallas import tpu as pltpu
from jax.sharding import PartitionSpec as P

DEPTH = 16


def combine_kernel(
    order, spots, bounds, front, panel, near, crossed, passed, assembled, partial, acc, held, total, sems
):
    step = pl.program_id(0)
    steps = pl.num_programs(0)
    tile = held.shape[2]
    n_here = acc.shape[0]
    cols_blocks = front.shape[2] // tile
    n_filled = bounds[steps]

    sources, first = [], 0
    for source in (near, crossed, passed):
        sources.append((source, first))
        first += source.shape[0]

    def fetch(e):
        slot = lax.rem(e, DEPTH)
        place = order[e]
        for source, first in sources:
            @pl.when((place >= first) & (place < first + source.shape[0]))
            def _():
                pltpu.make_async_copy(
                    source.at[place - first], held.at[slot], sems.at[slot]
                ).start()

    @pl.when(step == 0)
    def _():
        for e in range(DEPTH):
            @pl.when(e < n_filled)
            def _():
                fetch(e)

    for b in range(n_here):
        r, c = b // cols_blocks, b % cols_blocks
        acc[b] = front[:, r * tile:(r + 1) * tile, c * tile:(c + 1) * tile].astype(jnp.float32)

    def add(e, carry):
        slot = lax.rem(e, DEPTH)
        pltpu.make_async_copy(near.at[0], held.at[slot], sems.at[slot]).wait()
        b = spots[e] - step * n_here
        acc[b] = acc[b] + held[slot].astype(jnp.float32)

        @pl.when(e + DEPTH < n_filled)
        def _():
            fetch(e + DEPTH)

        return carry

    lax.fori_loop(bounds[step], bounds[step + 1], add, 0)

    for b in range(n_here):
        r, c = b // cols_blocks, b % cols_blocks
        assembled[:, r * tile:(r + 1) * tile, c * tile:(c + 1) * tile] = acc[b].astype(
            jnp.bfloat16
        )

    @pl.when(step == 0)
    def _():
        total[...] = jnp.zeros_like(total)

    def times(a, b):
        return lax.dot_general(
            a, b, (((0,), (0,)), ((), ())), preferred_element_type=jnp.float32
        )

    total[0] += times(panel[0], assembled[0]) + times(panel[1], assembled[1])
    total[1] += times(panel[0], assembled[1]) - times(panel[1], assembled[0])

    @pl.when(step == steps - 1)
    def _():
        rows_out = partial.shape[2]
        for d in range(partial.shape[0]):
            partial[d] = total[:, d * rows_out:(d + 1) * rows_out, :].astype(jnp.bfloat16)


def combine(front, panel, near, crossed, passed, order, spots, bounds, n_row, group):
    _, rows, width = front.shape
    p_size = panel.shape[2]
    tile = near.shape[2]
    high = group * tile
    steps = rows // high
    return pl.pallas_call(
        combine_kernel,
        grid_spec=pltpu.PrefetchScalarGridSpec(
            num_scalar_prefetch=3,
            grid=(steps,),
            in_specs=[
                pl.BlockSpec((2, high, width), lambda i, *_: (0, i, 0)),
                pl.BlockSpec((2, high, p_size), lambda i, *_: (0, i, 0)),
                pl.BlockSpec(memory_space=pl.ANY),
                pl.BlockSpec(memory_space=pl.ANY),
                pl.BlockSpec(memory_space=pl.ANY),
            ],
            out_specs=[
                pl.BlockSpec((2, high, width), lambda i, *_: (0, i, 0)),
                pl.BlockSpec((n_row, 2, p_size // n_row, width), lambda i, *_: (0, 0, 0, 0)),
            ],
            scratch_shapes=[
                pltpu.VMEM((group * (width // tile), 2, tile, tile), jnp.float32),
                pltpu.VMEM((DEPTH, 2, tile, tile), jnp.bfloat16),
                pltpu.VMEM((2, p_size, width), jnp.float32),
                pltpu.SemaphoreType.DMA((DEPTH,)),
            ],
        ),
        out_shape=[
            jax.ShapeDtypeStruct(front.shape, jnp.bfloat16),
            jax.ShapeDtypeStruct((n_row, 2, p_size // n_row, width), jnp.bfloat16),
        ],
        compiler_params=pltpu.CompilerParams(dimension_semantics=("arbitrary",)),
    )(order, spots, bounds, front, panel, near, crossed, passed)


def by_spot(got_spots, n_local, per_step):
    n = got_spots.shape[0]
    index = jnp.arange(n, dtype=jnp.int32)
    ahead = (got_spots[None, :] < got_spots[:, None]) | (
        (got_spots[None, :] == got_spots[:, None]) & (index[None, :] < index[:, None])
    )
    place = jnp.sum(ahead.astype(jnp.int32), axis=1)
    at = place[None, :] == index[:, None]
    order = jnp.sum(jnp.where(at, index[None, :], 0), axis=1)
    spots = jnp.sum(jnp.where(at, got_spots[None, :], 0), axis=1)
    edges = jnp.arange(n_local // per_step + 1, dtype=jnp.int32) * per_step
    bounds = jnp.sum((got_spots[None, :] < edges[:, None]).astype(jnp.int32), axis=1)
    return order, spots, bounds


def peers_in_turn(n):
    return sorted(range(1, n), key=lambda j: (bin(j).count("1"), -j))


def swap_kernel(n_half, n_col, slots, direct, length, *refs):
    if length:
        send, got, crossed, mirrored, send_sems, recv_sems = refs
    else:
        send, got, send_sems, recv_sems = refs
    row, col = lax.axis_index("row"), lax.axis_index("col")
    half_rows = n_half // n_col
    half = row // half_rows
    k = lax.rem(row, half_rows) * n_col + col
    even = n_half & (n_half - 1) == 0

    def peer(j):
        if not even:
            return lax.rem(k + j, n_half)
        place = k
        for b in range(n_half.bit_length() - 1):
            if j >> b & 1:
                place = place + (1 << b) * (1 - 2 * ((k // (1 << b)) % 2))
        return place

    def device(side, p):
        return (side * half_rows + p // n_col, lax.rem(p, n_col))

    mesh_id = pl.DeviceIdType.MESH
    barrier = pltpu.get_barrier_semaphore()
    for j in range(1, n_half):
        pl.semaphore_signal(
            barrier, inc=1, device_id=device(half, peer(j)), device_id_type=mesh_id
        )
    if length:
        for j in range(n_half):
            pl.semaphore_signal(
                barrier, inc=1, device_id=device(1 - half, peer(j)), device_id_type=mesh_id
            )
    pl.semaphore_wait(barrier, 2 * n_half - 1 if length else n_half - 1)

    copies = []

    def post(source, target, number, to):
        copies.append(
            pltpu.make_async_remote_copy(
                src_ref=source,
                dst_ref=target,
                send_sem=send_sems.at[number],
                recv_sem=recv_sems.at[number],
                device_id=to,
                device_id_type=mesh_id,
            )
        )

    def pieces(count):
        step = count // 2 if count % 2 == 0 else count
        return [(n, n * step, step) for n in range(count // step)]

    turn = peers_in_turn(n_half)
    if length:
        base = n_half * slots
        post(
            send.at[pl.ds(base + n_half * direct, length)],
            mirrored.at[pl.ds(0, length)],
            0,
            device(1 - half, k),
        )
        for n, first, step in pieces(direct):
            for j in [0] + turn:
                post(
                    send.at[pl.ds(base + peer(j) * direct + first, step)],
                    crossed.at[pl.ds(k * direct + first, step)],
                    2 * (n_half + j) + n,
                    device(1 - half, peer(j)),
                )
    for n, first, step in pieces(slots):
        for j in turn:
            post(
                send.at[pl.ds(peer(j) * slots + first, step)],
                got.at[pl.ds(k * slots + first, step)],
                2 * j + n,
                device(half, peer(j)),
            )
    for copy in copies:
        copy.start()
    own = pltpu.make_async_copy(
        send.at[pl.ds(k * slots, slots)],
        got.at[pl.ds(k * slots, slots)],
        send_sems.at[4 * n_half],
    )
    own.start()
    own.wait()
    for copy in copies:
        copy.wait()


def swap(send, n_half, n_col, slots, direct, room, length, number):
    def shape(rows):
        return jax.ShapeDtypeStruct((rows,) + send.shape[1:], send.dtype)

    shapes = [shape(n_half * slots)]
    if length:
        shapes += [shape(n_half * direct), shape(room)]
    return pl.pallas_call(
        functools.partial(swap_kernel, n_half, n_col, slots, direct, length),
        in_specs=[pl.BlockSpec(memory_space=pl.ANY)],
        out_specs=[pl.BlockSpec(memory_space=pl.ANY)] * len(shapes),
        out_shape=shapes,
        scratch_shapes=[
            pltpu.SemaphoreType.DMA((4 * n_half + 1,)),
            pltpu.SemaphoreType.DMA((4 * n_half,)),
        ],
        compiler_params=pltpu.CompilerParams(collective_id=number, has_side_effects=True),
    )(send)


def fold_kernel(n_row, part, out, sums, landed, send_sems, recv_sems):
    row, col = lax.axis_index("row"), lax.axis_index("col")
    bits = n_row.bit_length() - 1
    width = part.shape[3]

    def flip(t):
        place = row
        for b in range(bits):
            if t >> b & 1:
                place = place + (1 << b) * (1 - 2 * ((row // (1 << b)) % 2))
        return place

    mesh_id = pl.DeviceIdType.MESH
    barrier = pltpu.get_barrier_semaphore()
    for b in range(bits):
        pl.semaphore_signal(
            barrier, inc=1, device_id=(flip(1 << b), col), device_id_type=mesh_id
        )
    pl.semaphore_wait(barrier, bits)

    orders = [list(range(bits))]
    if width % 256 == 0 and bits > 1:
        orders.append([1, 0] + list(range(2, bits)))
    span = width // len(orders)
    left = [list(range(n_row)) for _ in orders]
    parts_of = [{t: [] for t in range(n_row)} for _ in orders]
    used = 0

    def value(h, t):
        total = part[flip(t), :, :, h * span:(h + 1) * span].astype(jnp.float32)
        for slot in parts_of[h][t]:
            total = total + landed[slot].astype(jnp.float32)
        return total

    for step in range(bits):
        copies = []
        for h, order in enumerate(orders):
            bit = 1 << order[step]
            for t in [t for t in left[h] if t & bit]:
                if step == 0:
                    source = part.at[flip(t), :, :, pl.ds(h * span, span)]
                else:
                    sums[used] = value(h, t).astype(jnp.bfloat16)
                    source = sums.at[used]
                copy = pltpu.make_async_remote_copy(
                    src_ref=source,
                    dst_ref=landed.at[used],
                    send_sem=send_sems.at[used],
                    recv_sem=recv_sems.at[used],
                    device_id=(flip(bit), col),
                    device_id_type=mesh_id,
                )
                copy.start()
                copies.append((copy, h, t ^ bit, used))
                used += 1
            left[h] = [t for t in left[h] if not t & bit]
        for copy, h, t, slot in copies:
            copy.wait()
            parts_of[h][t].append(slot)
    for h in range(len(orders)):
        out[:, :, h * span:(h + 1) * span] = value(h, 0)


def fold(partial, n_row, number):
    _, _, rows_out, width = partial.shape
    halves = 2 if width % 256 == 0 and n_row > 2 else 1
    count = halves * (n_row - 1)
    block = (count, 2, rows_out, width // halves)
    return pl.pallas_call(
        functools.partial(fold_kernel, n_row),
        in_specs=[pl.BlockSpec(memory_space=pltpu.VMEM)],
        out_specs=pl.BlockSpec(memory_space=pltpu.VMEM),
        out_shape=jax.ShapeDtypeStruct((2, rows_out, width), jnp.float32),
        scratch_shapes=[
            pltpu.VMEM(block, jnp.bfloat16),
            pltpu.VMEM(block, jnp.bfloat16),
            pltpu.SemaphoreType.DMA((count,)),
            pltpu.SemaphoreType.DMA((count,)),
        ],
        compiler_params=pltpu.CompilerParams(collective_id=number, has_side_effects=True),
    )(partial)


def body(front, child_tiles, tile_owner, tile_spot, tile_count, panel):
    n_row = lax.axis_size("row")
    n_col = lax.axis_size("col")
    n_dev = n_row * n_col
    n_half = n_dev // 2
    n_tiles = child_tiles.shape[0]
    tile = child_tiles.shape[2]
    slots = max(2, 2 * n_tiles // n_dev)
    direct = slots // 2
    beyond = slots - direct
    room = n_half * beyond
    near_rows = n_half * slots
    far_rows = n_half * direct
    rows_blocks = front.shape[1] // tile
    cols_blocks = front.shape[2] // tile
    n_local = rows_blocks * cols_blocks
    group = 2 if rows_blocks % 2 == 0 else 1
    half = lax.axis_index("row") // (n_row // 2)
    mine = lax.rem(lax.axis_index("row"), n_row // 2) * n_col + lax.axis_index("col")
    order = jnp.arange(n_tiles, dtype=jnp.int32)
    devices = jnp.arange(n_dev, dtype=jnp.int32)
    places = jnp.arange(n_half, dtype=jnp.int32)
    rows = jnp.arange(2 * near_rows, dtype=jnp.int32)
    owner = tile_owner[:, 0]
    live = order < tile_count[0]
    is_far = live & (owner // n_half != half)
    earlier = (owner[:, None] == owner[None, :]) & live[None, :] & (order[None, :] < order[:, None])
    rank = jnp.sum(earlier.astype(jnp.int32), axis=1)
    is_over = is_far & (rank >= direct)
    below = jnp.sum(
        (is_over[None, :] & (owner[None, :] < owner[:, None])).astype(jnp.int32), axis=1
    )
    spread = jnp.where(live, owner * slots + rank, 2 * near_rows)
    place = lax.rem(owner, n_half)
    packed = jnp.where(
        is_over,
        near_rows + far_rows + below + rank - direct,
        jnp.where(is_far, near_rows + place * direct + rank, place * slots + rank),
    )
    packed = jnp.where(live, packed, 2 * near_rows)
    picked = jnp.sum(jnp.where(packed[None, :] == rows[:, None], order[None, :], 0), axis=1)
    send_spots = n_local + jnp.sum(
        jnp.where(spread[None, :] == rows[:, None], tile_spot[None, :] - n_local, 0), axis=1
    )
    far_owner = jnp.where(is_over, place, n_half)
    far_counts = jnp.sum((far_owner[None, :] == places[:, None]).astype(jnp.int32), axis=1)
    news = jnp.concatenate(
        [
            send_spots.reshape(n_dev, slots),
            jnp.broadcast_to(far_counts[None, :], (n_dev, n_half)),
        ],
        axis=1,
    )
    heard = lax.all_to_all(news, ("row", "col"), split_axis=0, concat_axis=0, tiled=True)
    send = child_tiles[picked]
    fullest = jnp.max(jnp.sum(heard[:, slots:], axis=1))
    levels = sorted({-(-room * part // 16) for part in (5, 7, 16)})
    level = sum((fullest > size).astype(jnp.int32) for size in levels[:-1])
    near, crossed, mirrored = lax.switch(
        level,
        [
            functools.partial(
                lambda size, number, s: tuple(
                    swap(s, n_half, n_col, slots, direct, room, size, number)
                ),
                size,
                number,
            )
            for number, size in enumerate(levels)
        ],
        send,
    )
    across = (1 - half) * n_half + mine
    theirs = jnp.sum(
        jnp.where(devices[:, None] == across, heard[:, slots:], 0), axis=0
    )
    start = jnp.sum(jnp.where(places[None, :] < places[:, None], theirs[None, :], 0), axis=1)
    ranks = jnp.arange(beyond, dtype=jnp.int32)
    taken = jnp.where(ranks[None, :] < theirs[:, None], start[:, None] + ranks[None, :], 0)
    (passed,) = swap(
        mirrored[taken.reshape(room)], n_half, n_col, beyond, direct, room, 0, len(levels)
    )
    spots_in = heard[:, :slots].reshape(2, n_half, slots)
    spots_near = jnp.where(half == 0, spots_in[0], spots_in[1])
    spots_far = jnp.where(half == 0, spots_in[1], spots_in[0])
    got_spots = jnp.concatenate(
        [
            spots_near.reshape(near_rows),
            spots_far[:, :direct].reshape(far_rows),
            spots_far[:, direct:].reshape(room),
        ]
    )
    listed, spots, bounds = by_spot(got_spots, n_local, group * cols_blocks)
    assembled, partial = combine(
        front, panel, near, crossed, passed, listed, spots, bounds, n_row, group
    )
    sample = fold(partial, n_row, len(levels) + 1)
    return (assembled, sample)


def solution(mesh):
    placed = (
        P(None, "row", "col"),
        P(("row", "col"), None, None, None),
        P(("row", "col"), None),
        P(("row", "col")),
        P(("row", "col")),
        P(None, "row", None),
    )
    return jax.shard_map(
        body,
        mesh=mesh,
        in_specs=placed,
        out_specs=(P(None, "row", "col"), P(None, "row", "col")),
        check_vma=False,
    )
```
